256 devices in a mesh: dp: 2 (over z_hi), context: 8 (over y, core), tensor: 16 (over z_lo, x).
Axes of the slice: x: 4, y: 4, z: 8 (z_hi: 2, z_lo: 4; z = z_hi * 4 + z_lo), core: 2. Of those that a mesh axis runs over, the one named last changes fastest.
Arguments:
- tokens: bfloat16 [2, 4096, 5376], P('dp', ('context', 'tensor')), may hold values from -48 to 48
- output_gradient: bfloat16 [2, 4096, 5376], P('dp', ('context', 'tensor')), may hold values from -48 to 48
- document_index: int32 [2, 4096], P('dp'), may hold values from 0 to 3, never falling along the last dimension, each value on 1 to 2048 neighbouring positions
- query_weight: bfloat16 [5376, 4096], P(None, 'tensor'), may hold values from -1 to 1
- key_value_weight: bfloat16 [2, 5376, 2048], P(None, None, 'tensor'), may hold values from -1 to 1
- output_weight: bfloat16 [4096, 5376], P('tensor'), may hold values from -0.09375 to 0.09375
- adapter_down_projections: bfloat16 [3, 16, 5376], replicated, may hold values from -0.078125 to 0.078125
- adapter_up_query: bfloat16 [16, 4096], P(None, 'tensor'), may hold values from -0.29882812 to 0.29882812
- adapter_up_key_value: bfloat16 [2, 16, 2048], P(None, None, 'tensor'), may hold values from -0.29882812 to 0.29882812
- adapter_down_output: bfloat16 [16, 4096], P(None, 'tensor'), may hold values from -0.09375 to 0.09375
- adapter_up_output: bfloat16 [16, 5376], replicated, may hold values from -0.29882812 to 0.29882812
Outputs:
- grad_input: bfloat16 [2, 4096, 5376], P('dp', ('context', 'tensor'))
- grad_down_qkv: float32 [3, 16, 5376], replicated
- query_up_gradient: float32 [16, 4096], P(None, 'tensor')
- grad_up_keyvalue: float32 [2, 16, 2048], P(None, None, 'tensor')
- grad_down_out: float32 [16, 4096], P(None, 'tensor')
- output_up_gradient: float32 [16, 5376], replicated
The draws below stay inside these ranges and needn't reach their ends.
Inputs may be any that keep to these rules, and one draw needn't show every extreme that they name: `document_index`: ids never fall along a sequence; each document holds 1 to half of 4096 tokens, and one holds exactly that many.
All inputs are finite; a program needn't handle non-finite values.
Results may differ from the reference program's by a relative error of at most 0.03.
Values may be sent and summed in bfloat16 or wider, within the bound.
No kernel may reach another device: no remote copies, remote signals or barrier semaphores. Data moves between devices by JAX's collectives and lax.ppermute only.
A program may use at most 128 MiB of HBM per device.

```python
import math
import jax
import jax.numpy as jnp
import numpy as np
from jax import lax

MODEL_DIM = 5376
QUERY_HEADS = 32
KEY_VALUE_HEADS = 16
HEAD_SIZE = 128
WINDOW = 1024
ADAPTER_RANK = 16
CTX_TOK = 512
SEQUENCE_TOKENS = 4096
SEQS = 2
HALO = 2
N_CONTEXT = 8
N_TENSOR = 16


def projection_tables(key):
    common_term = jax.random.truncated_normal(jax.random.fold_in(key, 11), -6.0, 6.0, (2, MODEL_DIM, KEY_VALUE_HEADS, HEAD_SIZE), jnp.float32)
    self_term = jax.random.truncated_normal(jax.random.fold_in(key, 12), -6.0, 6.0, (MODEL_DIM, KEY_VALUE_HEADS, QUERY_HEADS // KEY_VALUE_HEADS, HEAD_SIZE), jnp.float32)
    query_table = self_term
    query_table = query_table.reshape(MODEL_DIM, QUERY_HEADS * HEAD_SIZE) * MODEL_DIM ** (-0.5)
    key_value_matrix = common_term.reshape(2, MODEL_DIM, KEY_VALUE_HEADS * HEAD_SIZE) * MODEL_DIM ** (-0.5)
    return (jnp.clip(query_table, -1.0, 1.0), jnp.clip(key_value_matrix, -1.0, 1.0))


def draw_query_weight(key, part):
    return projection_tables(key)[0].astype(jnp.bfloat16)


def draw_key_value_weight(key, part):
    return projection_tables(key)[1].astype(jnp.bfloat16)


def draw_tokens(key, part):
    sample = jax.random.truncated_normal(jax.random.fold_in(key, 21), -6.0, 6.0, (SEQS, SEQUENCE_TOKENS, MODEL_DIM), jnp.float32)
    return jnp.clip(sample, -48.0, 48.0).astype(jnp.bfloat16)


def block_scale(key, extent, shards, smallest, top_value):
    loudness = 1.0
    for axis_at, blocks in shards:
        heights = jax.random.uniform(jax.random.fold_in(jax.random.fold_in(key, 6), axis_at), (blocks,), jnp.float32, smallest / len(shards), top_value / len(shards))
        loudness = loudness * jnp.repeat(jnp.exp(heights), extent[axis_at] // blocks).reshape((-1,) + (1,) * (len(extent) - 1 - axis_at))
    return loudness


def profile(number_of, total, reach, slope):
    loads = [(1 << 20) // math.isqrt(standing ** slope) + 1 for standing in range(2, number_of + 1)]
    surplus, holding = total - reach - (number_of - 1), [1] * (number_of - 1)
    while surplus > 0:
        free = [i for i in range(number_of - 1) if holding[i] < reach]
        whole, remaining = sum([loads[i] for i in free]), surplus
        for i in free:
            addition = min(reach - holding[i], max(1, remaining * loads[i] // whole), surplus)
            holding[i] = holding[i] + addition
            surplus = surplus - addition
    return np.array([reach] + holding)


def uneven(stream_key, amount, total, bound, slope):
    if amount == 2:
        one = jax.random.randint(stream_key, (), max(1, total - bound), min(bound, total - 1) + 1)
        return jnp.stack([one, total - one])
    tallies = jnp.asarray(profile(amount, total, bound, slope), jnp.int32)
    pairs = (amount - 1) // 2
    donor, receiver = tallies[1:1 + 2 * pairs:2], tallies[2:2 + 2 * pairs:2]
    margin = jnp.minimum(donor - 1, bound - receiver)
    shifted = jax.random.randint(jax.random.fold_in(stream_key, 1), (pairs,), 0, 1 << 20) % (margin + 1)
    tallies = tallies.at[1:1 + 2 * pairs:2].set(donor - shifted).at[2:2 + 2 * pairs:2].set(receiver + shifted)
    return tallies[jax.random.permutation(jax.random.fold_in(stream_key, 2), amount)]


def scatter_about(stream_key, extent, spread, bound, split=(), kind=jnp.bfloat16):
    array = jax.random.normal(stream_key, extent, jnp.float32) * spread
    if len(split) > 0:
        array = block_scale(stream_key, extent, split, -0.22, 0.18) * array
    return jnp.clip(array, min=-bound, max=bound).astype(kind)


def setup_inputs(seed: int = 0) -> dict:
    seeds = jax.random.split(jax.random.key(seed), 12)
    tokens = draw_tokens(jax.random.fold_in(seeds[11], 71), 0)
    output_gradient = scatter_about(seeds[1], (SEQS, SEQUENCE_TOKENS, MODEL_DIM), 8.0, 48.0, ((0, 2), (1, 128)))
    document_index = jax.vmap(lambda own: jnp.searchsorted(jnp.cumsum(uneven(own, 4, SEQUENCE_TOKENS, SEQUENCE_TOKENS // 2, 1)), jnp.arange(SEQUENCE_TOKENS), side="right"))(jax.random.split(seeds[2], SEQS)).reshape((SEQS, SEQUENCE_TOKENS)).astype(jnp.int32)
    query_weight = draw_query_weight(jax.random.fold_in(seeds[11], 71), 0)
    key_value_weight = draw_key_value_weight(jax.random.fold_in(seeds[11], 71), 0)
    output_weight = scatter_about(seeds[5], (QUERY_HEADS * HEAD_SIZE, MODEL_DIM), (QUERY_HEADS * HEAD_SIZE) ** -0.5, 0.09375, ((0, 16),))
    adapter_down_projections = scatter_about(seeds[6], (3, ADAPTER_RANK, MODEL_DIM), MODEL_DIM ** -0.5, 0.078125)
    adapter_up_query = scatter_about(seeds[7], (ADAPTER_RANK, QUERY_HEADS * HEAD_SIZE), 0.05, 0.29882812, ((1, 16),))
    adapter_up_key_value = scatter_about(seeds[8], (2, ADAPTER_RANK, KEY_VALUE_HEADS * HEAD_SIZE), 0.05, 0.29882812, ((2, 16),))
    adapter_down_output = scatter_about(seeds[9], (ADAPTER_RANK, QUERY_HEADS * HEAD_SIZE), (QUERY_HEADS * HEAD_SIZE) ** -0.5, 0.09375, ((1, 16),))
    adapter_up_output = scatter_about(seeds[10], (ADAPTER_RANK, MODEL_DIM), 0.05, 0.29882812)
    return {"tokens": tokens, "output_gradient": output_gradient, "document_index": document_index, "query_weight": query_weight, "key_value_weight": key_value_weight, "output_weight": output_weight, "adapter_down_projections": adapter_down_projections, "adapter_up_query": adapter_up_query, "adapter_up_key_value": adapter_up_key_value, "adapter_down_output": adapter_down_output, "adapter_up_output": adapter_up_output}


adapter_scale = 2.0
attn_scale = 168.0 ** -0.5
rope_base = 10000.0


def rope_tables(positions, head_width):
    half_width = head_width // 2
    inverse = rope_base ** (-(jnp.arange(half_width, dtype=jnp.float32) * 2.0 / head_width))
    angle = positions[:, None] * inverse[None, :]
    return jnp.cos(angle), jnp.sin(angle)


def apply_rotation(vectors, cosine_table, sine_values):
    half_width = vectors.shape[-1] // 2
    front_half = vectors[..., :half_width]
    back_half = vectors[..., half_width:]
    cosine_table = cosine_table[:, None, :]
    sine_values = sine_values[:, None, :]
    return jnp.concatenate([front_half * cosine_table - back_half * sine_values, back_half * cosine_table + front_half * sine_values], -1)


def undo_rotation(grads, cosine_table, sine_values):
    half_width = grads.shape[-1] // 2
    front_half = grads[..., :half_width]
    back_half = grads[..., half_width:]
    cosine_table = cosine_table[:, None, :]
    sine_values = sine_values[:, None, :]
    return jnp.concatenate([front_half * cosine_table + back_half * sine_values, back_half * cosine_table - front_half * sine_values], -1)


def to_low(values_high):
    return lax.optimization_barrier(values_high.astype(jnp.bfloat16)).astype(jnp.float32)


def band_block(queries, key_rows, value_rows, attention_output_gradient, allowed):
    row_count, heads_q, head_width = queries.shape
    heads_kv = key_rows.shape[1]
    group_size = heads_q // heads_kv
    query_groups = queries.astype(jnp.float32).reshape(row_count, heads_kv, group_size, head_width)
    grad_groups = attention_output_gradient.astype(jnp.float32).reshape(row_count, heads_kv, group_size, head_width)
    key_high = key_rows.astype(jnp.float32)
    value_high = value_rows.astype(jnp.float32)
    scores = jnp.einsum("chgd,khd->hgck", query_groups, key_high) * attn_scale
    scores = jnp.where(allowed[None, None], scores, -1e30)
    row_max = jnp.max(scores, -1, keepdims=True)
    exponent = jnp.exp(scores - row_max)
    weights = exponent / jnp.sum(exponent, -1, keepdims=True)
    weights_low = to_low(weights)
    attention_output = to_low(jnp.einsum("hgck,khd->chgd", weights_low, value_high))
    grad_weights = jnp.einsum("chgd,khd->hgck", grad_groups, value_high)
    row_dot = jnp.einsum("chgd,chgd->hgc", grad_groups, attention_output)
    grad_scores = to_low(weights * (grad_weights - row_dot[..., None]) * attn_scale)
    query_gradient = jnp.einsum("hgck,khd->chgd", grad_scores, key_high)
    key_gradient = jnp.einsum("hgck,chgd->khd", grad_scores, query_groups)
    value_gradient = jnp.einsum("hgck,chgd->khd", weights_low, grad_groups)
    return (attention_output.astype(jnp.bfloat16).reshape(row_count, heads_q, head_width),
            query_gradient.reshape(row_count, heads_q, head_width), key_gradient, value_gradient)


def reference(tokens, output_gradient, document_index, query_weight, key_value_weight, output_weight, adapter_down_projections, adapter_up_query, adapter_up_key_value, adapter_down_output, adapter_up_output):
    shard_len = CTX_TOK
    padding_length = HALO * shard_len
    query_columns = QUERY_HEADS * HEAD_SIZE // N_TENSOR
    key_value_columns = KEY_VALUE_HEADS * HEAD_SIZE // N_TENSOR
    down_factors_all = adapter_down_projections.reshape(3 * ADAPTER_RANK, MODEL_DIM)
    cosine_table, sine_values = rope_tables(jnp.arange(SEQUENCE_TOKENS).astype(jnp.float32), HEAD_SIZE)
    outputs = []
    grad_down_total = jnp.zeros((3 * ADAPTER_RANK, MODEL_DIM), jnp.float32)
    query_up_gradient = jnp.zeros((ADAPTER_RANK, QUERY_HEADS * HEAD_SIZE), jnp.float32)
    key_up_gradient = jnp.zeros((ADAPTER_RANK, KEY_VALUE_HEADS * HEAD_SIZE), jnp.float32)
    value_up_gradient = jnp.zeros((ADAPTER_RANK, KEY_VALUE_HEADS * HEAD_SIZE), jnp.float32)
    grad_down_out = jnp.zeros((ADAPTER_RANK, QUERY_HEADS * HEAD_SIZE), jnp.float32)
    output_up_gradient = jnp.zeros((ADAPTER_RANK, MODEL_DIM), jnp.float32)
    for sequence in range(SEQS):
        input_tokens = tokens[sequence]
        incoming_gradient = output_gradient[sequence]
        segment_row = document_index[sequence]
        adapted = jnp.dot(input_tokens, down_factors_all.T, preferred_element_type=jnp.float32).astype(jnp.bfloat16)
        adapted_query = adapted[:, :ADAPTER_RANK]
        adapted_key = adapted[:, ADAPTER_RANK:2 * ADAPTER_RANK]
        adapted_value = adapted[:, 2 * ADAPTER_RANK:]
        query_linear = jnp.dot(input_tokens, query_weight, preferred_element_type=jnp.float32) + adapter_scale * jnp.dot(adapted_query, adapter_up_query, preferred_element_type=jnp.float32)
        key_linear = jnp.dot(input_tokens, key_value_weight[0], preferred_element_type=jnp.float32) + adapter_scale * jnp.dot(adapted_key, adapter_up_key_value[0], preferred_element_type=jnp.float32)
        value_linear = jnp.dot(input_tokens, key_value_weight[1], preferred_element_type=jnp.float32) + adapter_scale * jnp.dot(adapted_value, adapter_up_key_value[1], preferred_element_type=jnp.float32)
        queries = apply_rotation(query_linear.reshape(SEQUENCE_TOKENS, QUERY_HEADS, HEAD_SIZE), cosine_table, sine_values).astype(jnp.bfloat16)
        key_full = apply_rotation(key_linear.reshape(SEQUENCE_TOKENS, KEY_VALUE_HEADS, HEAD_SIZE), cosine_table, sine_values).astype(jnp.bfloat16)
        value_full = value_linear.reshape(SEQUENCE_TOKENS, KEY_VALUE_HEADS, HEAD_SIZE).astype(jnp.bfloat16)
        up_gradient = (adapter_scale * jnp.dot(incoming_gradient, adapter_up_output.T, preferred_element_type=jnp.float32)).astype(jnp.bfloat16)
        attention_output_gradient = (jnp.dot(incoming_gradient, output_weight.T, preferred_element_type=jnp.float32) + jnp.dot(up_gradient, adapter_down_output, preferred_element_type=jnp.float32)).astype(jnp.bfloat16)
        attention_output_gradient = attention_output_gradient.reshape(SEQUENCE_TOKENS, QUERY_HEADS, HEAD_SIZE)
        key_padded = jnp.concatenate([jnp.zeros((padding_length, KEY_VALUE_HEADS, HEAD_SIZE), jnp.bfloat16), key_full], 0)
        value_padded = jnp.concatenate([jnp.zeros((padding_length, KEY_VALUE_HEADS, HEAD_SIZE), jnp.bfloat16), value_full], 0)
        segment_pad = jnp.concatenate([jnp.full((padding_length,), -1, jnp.int32), segment_row.astype(jnp.int32)], 0)

        def one_block(block_at):
            begin_at = (block_at * shard_len).astype(jnp.int32)
            query_part = lax.dynamic_slice_in_dim(queries, begin_at, shard_len, 0)
            grad_part = lax.dynamic_slice_in_dim(attention_output_gradient, begin_at, shard_len, 0)
            key_part = lax.dynamic_slice_in_dim(key_padded, begin_at, padding_length + shard_len, 0)
            value_part = lax.dynamic_slice_in_dim(value_padded, begin_at, padding_length + shard_len, 0)
            key_seg = lax.dynamic_slice_in_dim(segment_pad, begin_at, padding_length + shard_len, 0)
            query_seg = lax.dynamic_slice_in_dim(segment_row.astype(jnp.int32), begin_at, shard_len, 0)
            query_pos = begin_at + jnp.arange(shard_len, dtype=jnp.int32)
            key_pos = begin_at - padding_length + jnp.arange(padding_length + shard_len, dtype=jnp.int32)
            offset = query_pos[:, None] - key_pos[None, :]
            allowed = (key_pos >= 0)[None, :] & (offset >= 0) & (offset < WINDOW) & (query_seg[:, None] == key_seg[None, :])
            return band_block(query_part, key_part, value_part, grad_part, allowed)

        attention_output, grad_query_rot, grad_key_parts, grad_value_parts = lax.map(one_block, jnp.arange(N_CONTEXT, dtype=jnp.int32))
        pair_parts = jnp.stack([grad_key_parts, grad_value_parts], 1)

        def extra_term(block_at, running):
            begin_at = (block_at * shard_len).astype(jnp.int32)
            current = lax.dynamic_slice_in_dim(running, begin_at, padding_length + shard_len, 1)
            return lax.dynamic_update_slice_in_dim(running, current + pair_parts[block_at], begin_at, 1)

        pairwise_total = lax.fori_loop(0, N_CONTEXT, extra_term, jnp.zeros((2, padding_length + SEQUENCE_TOKENS, KEY_VALUE_HEADS, HEAD_SIZE), jnp.float32))
        pairwise_total = pairwise_total[:, padding_length:]
        attention_output = attention_output.reshape(SEQUENCE_TOKENS, QUERY_HEADS * HEAD_SIZE)
        query_gradient = undo_rotation(grad_query_rot.reshape(SEQUENCE_TOKENS, QUERY_HEADS, HEAD_SIZE), cosine_table, sine_values).reshape(SEQUENCE_TOKENS, QUERY_HEADS * HEAD_SIZE).astype(jnp.bfloat16)
        key_gradient = undo_rotation(pairwise_total[0], cosine_table, sine_values).reshape(SEQUENCE_TOKENS, KEY_VALUE_HEADS * HEAD_SIZE).astype(jnp.bfloat16)
        value_gradient = pairwise_total[1].reshape(SEQUENCE_TOKENS, KEY_VALUE_HEADS * HEAD_SIZE).astype(jnp.bfloat16)
        factor_value = jnp.dot(attention_output, adapter_down_output.T, preferred_element_type=jnp.float32).astype(jnp.bfloat16)
        output_up_gradient = output_up_gradient + adapter_scale * jnp.dot(factor_value.T, incoming_gradient, preferred_element_type=jnp.float32)
        grad_down_out = grad_down_out + jnp.dot(up_gradient.T, attention_output, preferred_element_type=jnp.float32)
        query_up_gradient = query_up_gradient + adapter_scale * jnp.dot(adapted_query.T, query_gradient, preferred_element_type=jnp.float32)
        key_up_gradient = key_up_gradient + adapter_scale * jnp.dot(adapted_key.T, key_gradient, preferred_element_type=jnp.float32)
        value_up_gradient = value_up_gradient + adapter_scale * jnp.dot(adapted_value.T, value_gradient, preferred_element_type=jnp.float32)
        input_total = jnp.zeros((SEQUENCE_TOKENS, MODEL_DIM), jnp.float32)
        for group_index in range(N_TENSOR):
            query_lowrank = group_index * query_columns
            key_value_lowrank = group_index * key_value_columns
            query_gradient_grouped = query_gradient[:, query_lowrank:query_lowrank + query_columns]
            key_gradient_grouped = key_gradient[:, key_value_lowrank:key_value_lowrank + key_value_columns]
            value_gradient_grouped = value_gradient[:, key_value_lowrank:key_value_lowrank + key_value_columns]
            query_hidden = (adapter_scale * jnp.dot(query_gradient_grouped, adapter_up_query[:, query_lowrank:query_lowrank + query_columns].T, preferred_element_type=jnp.float32)).astype(jnp.bfloat16)
            key_hidden = (adapter_scale * jnp.dot(key_gradient_grouped, adapter_up_key_value[0][:, key_value_lowrank:key_value_lowrank + key_value_columns].T, preferred_element_type=jnp.float32)).astype(jnp.bfloat16)
            value_hidden = (adapter_scale * jnp.dot(value_gradient_grouped, adapter_up_key_value[1][:, key_value_lowrank:key_value_lowrank + key_value_columns].T, preferred_element_type=jnp.float32)).astype(jnp.bfloat16)
            hidden_all = jnp.concatenate([query_hidden, key_hidden, value_hidden], 1)
            grad_down_total = grad_down_total + jnp.dot(hidden_all.T, input_tokens, preferred_element_type=jnp.float32)
            term = jnp.dot(query_gradient_grouped, query_weight[:, query_lowrank:query_lowrank + query_columns].T, preferred_element_type=jnp.float32)
            term = term + jnp.dot(key_gradient_grouped, key_value_weight[0][:, key_value_lowrank:key_value_lowrank + key_value_columns].T, preferred_element_type=jnp.float32)
            term = term + jnp.dot(value_gradient_grouped, key_value_weight[1][:, key_value_lowrank:key_value_lowrank + key_value_columns].T, preferred_element_type=jnp.float32)
            term = term + jnp.dot(hidden_all, down_factors_all, preferred_element_type=jnp.float32)
            input_total = input_total + to_low(term)
        outputs.append(input_total.astype(jnp.bfloat16))
    grad_input = jnp.stack(outputs, 0)
    return (grad_input, grad_down_total.reshape(3, ADAPTER_RANK, MODEL_DIM), query_up_gradient,
            jnp.stack([key_up_gradient, value_up_gradient], 0), grad_down_out, output_up_gradient)
```

```python
import jax
import jax.numpy as jnp
import numpy as np
from jax import lax
from jax.sharding import PartitionSpec as P

HEAD_SIZE = 128
WINDOW = 1024
COLS = 384

adapter_scale = 2.0
attn_scale = 168.0 ** (-0.5)
rope_base = 10000.0
bf16 = jnp.bfloat16
f32 = jnp.float32


NEXT = {0: 2, 2: 3, 3: 1, 1: 0}
PREV = {v: k for k, v in NEXT.items()}


def route(f):
    pairs = []
    for z in range(4):
        for x in range(4):
            a, b = f(z, x)
            pairs.append((z * 4 + x, a * 4 + b))
    return pairs


XP = route(lambda z, x: (z, (x + 1) % 4))
XM = route(lambda z, x: (z, (x - 1) % 4))
X2 = route(lambda z, x: (z, (x + 2) % 4))
ZF = route(lambda z, x: (NEXT[z], x))
ZR = route(lambda z, x: (PREV[z], x))
ZF2 = route(lambda z, x: (NEXT[NEXT[z]], x))
BX1 = route(lambda z, x: (z, x ^ 1))
BZ1 = route(lambda z, x: (z ^ 1, x))
BZ2 = route(lambda z, x: (z ^ 2, x))
BACK = np.zeros((4, 4), np.int32)
for z0 in range(4):
    at = z0
    for k0 in range(4):
        BACK[z0, k0] = at
        at = PREV[at]


def send(v, perm, name, axis="tensor"):
    with jax.named_scope(name):
        return lax.ppermute(v, axis, perm)


def row_slots():
    ks, ms, rs = [], [], []

    def put(k, m, rows):
        for r in rows:
            ks.append(k)
            ms.append(m)
            rs.append(r)

    for k in range(4):
        for m in range(4):
            put(k, m, range(0, 8))
    for g in range(2):
        for m in (0, 1):
            for k in (2 * g, 2 * g + 1):
                put(k, m, range(8, 32))
        put(2 * g, 2, range(8, 32))
        put(2 * g + 1, 2, range(8, 32))
        for k in (2 * g, 2 * g + 1):
            put(k, 3, range(8, 32))
    return np.array(ks), np.array(ms), np.array(rs)


KS, MS, RS = row_slots()


def gather_rows(block, tag):
    a, b = block[:8], block[8:]
    bs = [b]
    for i in range(3):
        bs.append(send(bs[-1], ZF, f"{tag}bz{i}"))
    a1 = send(a, XP, f"{tag}ax1")
    a3 = send(a, XM, f"{tag}ax3")
    a2 = send(a, X2, f"{tag}ax2")
    parts = [jnp.concatenate([a, a1, a2, a3])]
    for i in range(3):
        parts.append(send(parts[-1], ZF, f"{tag}az{i}"))
    for g in range(2):
        own = jnp.concatenate(bs[2 * g : 2 * g + 2])
        left = send(own, XP, f"{tag}bx{g}l")
        right = send(own, XM, f"{tag}bx{g}r")
        top = send(left[:24], XP, f"{tag}bx{g}t")
        bottom = send(right[24:], XM, f"{tag}bx{g}b")
        parts += [own, left, top, bottom, right]
    return jnp.concatenate(parts)


def total(*terms):
    s = terms[0].astype(f32)
    for v in terms[1:]:
        s = s + v.astype(f32)
    return s.astype(bf16)


def scatter_rows(t, tag):
    w = send(t[96:128], ZR, f"{tag}az0")
    w = send(total(t[64:96], w), ZR, f"{tag}az1")
    w = send(total(t[32:64], w), ZR, f"{tag}az2")
    agg = total(t[0:32], w)
    done = [None] * 4
    for g in (1, 0):
        u = t[128 + 192 * g : 128 + 192 * (g + 1)]
        u0, u1, u2, u3 = u[:48], u[48:96], u[96:144], u[144:]
        s1 = send(u2[:24], XM, f"{tag}bx{g}t")
        s2 = send(u2[24:], XP, f"{tag}bx{g}b")
        u1 = jnp.concatenate([total(u1[:24], s1), u1[24:]])
        u3 = jnp.concatenate([u3[:24], total(u3[24:], s2)])
        v1 = send(u1, XM, f"{tag}bx{g}l")
        v3 = send(u3, XP, f"{tag}bx{g}r")
        r = total(u0, v1, v3)
        done[2 * g], done[2 * g + 1] = r[:24], r[24:]
    w = send(done[3], ZR, f"{tag}bz0")
    w = send(total(done[2], w), ZR, f"{tag}bz1")
    w = send(total(done[1], w), ZR, f"{tag}bz2")
    b = total(done[0], w)
    a = total(
        agg[:8],
        send(agg[8:16], XM, f"{tag}ax1"),
        send(agg[24:32], XP, f"{tag}ax3"),
        send(agg[16:24], X2, f"{tag}ax2"),
    )
    return jnp.concatenate([a, b])


def butterfly(v, steps, tag):
    for i, (axis, perm) in enumerate(steps):
        v = lax.optimization_barrier(v)
        v = total(v, send(v, perm, f"{tag}{i}", axis))
    return v


def rotate(v, cos, sin, sign):
    a, b = v[:, :64], v[:, 64:]
    return jnp.concatenate([a * cos - sign * (b * sin), b * cos + sign * (a * sin)], -1)


def dot(a, b):
    return jnp.dot(a, b, preferred_element_type=f32)


def dot_t(a, b):
    return lax.dot_general(a, b, (((1,), (1,)), ((), ())), preferred_element_type=f32)


def t_dot(a, b):
    return lax.dot_general(a, b, (((0,), (0,)), ((), ())), preferred_element_type=f32)


def local(
    tokens,
    output_gradient,
    document_index,
    query_weight,
    key_value_weight,
    output_weight,
    adapter_down_projections,
    adapter_up_query,
    adapter_up_key_value,
    adapter_down_output,
    adapter_up_output,
):
    c = lax.axis_index("context")
    t = lax.axis_index("tensor")
    z, x = t // 4, t % 4
    width = tokens.shape[2]
    shard = 512
    n_ctx = lax.axis_size("context")

    back = jnp.asarray(BACK)[z]
    zrow = jnp.where(KS == 0, back[0], jnp.where(KS == 1, back[1], jnp.where(KS == 2, back[2], back[3])))
    local_pos = (zrow * 4 + (x - jnp.asarray(MS, jnp.int32)) % 4) * 32 + jnp.asarray(RS, jnp.int32)
    q_pos = c * shard + local_pos
    key_pos = jnp.concatenate([q_pos - 2 * shard, q_pos - shard, q_pos])
    seg = document_index[0]
    low = jnp.maximum(q_pos - (WINDOW - 1), 0)
    for v in (1, 2, 3):
        start = jnp.sum((seg < v).astype(jnp.int32))
        low = jnp.maximum(low, jnp.where(start <= q_pos, start, 0))
    allowed = (key_pos[None, :] >= low[:, None]) & (key_pos[None, :] <= q_pos[:, None])
    inverse = rope_base ** (-(jnp.arange(64, dtype=f32) * 2.0 / HEAD_SIZE))
    angle = q_pos.astype(f32)[:, None] * inverse[None, :]
    cos, sin = jnp.cos(angle), jnp.sin(angle)

    down_all = adapter_down_projections.reshape(48, width)
    w_all = jnp.concatenate(
        [query_weight, key_value_weight[0], key_value_weight[1], down_all.T], 1
    )
    w_out = jnp.concatenate([output_weight, adapter_up_output], 0)

    xg = gather_rows(tokens[0], "xg_")
    gg = gather_rows(output_gradient[0], "gg_")

    lin = dot(xg, w_all)
    adapted = lin[:, 512:].astype(bf16)
    aq, ak, av = adapted[:, :16], adapted[:, 16:32], adapted[:, 32:]
    q_lin = lin[:, :256] + adapter_scale * dot(aq, adapter_up_query)
    k_lin = lin[:, 256:384] + adapter_scale * dot(ak, adapter_up_key_value[0])
    v_lin = lin[:, 384:512] + adapter_scale * dot(av, adapter_up_key_value[1])
    q = [rotate(q_lin[:, h * 128 : h * 128 + 128], cos, sin, 1.0).astype(bf16) for h in (0, 1)]
    k_own = rotate(k_lin, cos, sin, 1.0).astype(bf16)
    kv_own = jnp.stack([k_own, v_lin.astype(bf16)])
    kv_1 = send(kv_own, [(i, i + 1) for i in range(n_ctx - 1)], "halo1", "context")
    kv_2 = send(kv_own, [(i, i + 2) for i in range(n_ctx - 2)], "halo2", "context")
    kv = jnp.concatenate([kv_2, kv_1, kv_own], 1)
    keys, values = kv[0], kv[1]

    weights, low_weights, attended = [], [], []
    for h in (0, 1):
        s = jnp.where(allowed, dot_t(q[h], keys) * attn_scale, -1e30)
        e = jnp.exp(s - jnp.max(s, -1, keepdims=True))
        w = e / jnp.sum(e, -1, keepdims=True)
        weights.append(w)
        low_weights.append(w.astype(bf16))
        attended.append(dot(low_weights[h], values).astype(bf16))
    attended_all = jnp.concatenate(attended, 1)
    factor_part = dot_t(attended_all, adapter_down_output).astype(bf16)

    go = dot_t(gg, w_out)
    up_grad = (adapter_scale * go[:, 256:]).astype(bf16)
    d_out = (go[:, :256] + dot(up_grad, adapter_down_output)).astype(bf16)

    dq, dk, dv = [], 0.0, 0.0
    for h in (0, 1):
        do = d_out[:, h * 128 : h * 128 + 128]
        dw = dot_t(do, values)
        row = jnp.sum(do.astype(f32) * attended[h].astype(f32), -1, keepdims=True)
        ds = (weights[h] * (dw - row) * attn_scale).astype(bf16)
        dq.append(rotate(dot(ds, keys), cos, sin, -1.0).astype(bf16))
        dk = dk + t_dot(ds, q[h])
        dv = dv + t_dot(low_weights[h], do)
    dkv = jnp.stack([dk, dv])
    far = send(dkv[:, :shard].astype(bf16), [(i, i - 2) for i in range(2, n_ctx)], "back2", "context")
    near = send(dkv[:, shard : 2 * shard].astype(bf16), [(i, i - 1) for i in range(1, n_ctx)], "back1", "context")
    dkv = dkv[:, 2 * shard :] + far.astype(f32) + near.astype(f32)
    d_q = jnp.concatenate(dq, 1)
    d_k = rotate(dkv[0], cos, sin, -1.0).astype(bf16)
    d_v = dkv[1].astype(bf16)
    hidden = jnp.concatenate(
        [
            adapter_scale * dot_t(d_q, adapter_up_query),
            adapter_scale * dot_t(d_k, adapter_up_key_value[0]),
            adapter_scale * dot_t(d_v, adapter_up_key_value[1]),
        ],
        1,
    ).astype(bf16)

    term = dot_t(jnp.concatenate([d_q, d_k, d_v, hidden], 1), w_all).astype(bf16)
    grad_input = scatter_rows(term, "rs_")[None]

    order = (local_pos[None, :] == jnp.arange(shard, dtype=jnp.int32)[:, None]).astype(bf16)
    low_rank = dot(order, jnp.concatenate([hidden, factor_part], 1)).astype(bf16)
    low_rank = butterfly(
        low_rank, [("tensor", BX1), ("tensor", X2), ("tensor", BZ1), ("tensor", BZ2)], "lt"
    )
    low_rank = t_dot(order, low_rank).astype(bf16)
    first = jnp.minimum(t, width // COLS - 1) * COLS
    x_cols = lax.dynamic_slice_in_dim(xg, first, COLS, 1)
    g_cols = lax.dynamic_slice_in_dim(gg, first, COLS, 1)
    down_cols = t_dot(low_rank[:, :48], x_cols)
    up_cols = adapter_scale * t_dot(low_rank[:, 48:], g_cols)
    q_up = adapter_scale * t_dot(aq, d_q)
    k_up = adapter_scale * t_dot(ak, d_k)
    v_up = adapter_scale * t_dot(av, d_v)
    down_out = t_dot(up_grad, attended_all)
    small = jnp.concatenate(
        [
            down_cols.reshape(-1, 128),
            up_cols.reshape(-1, 128),
            q_up.reshape(-1, 128),
            k_up,
            v_up,
            down_out.reshape(-1, 128),
        ],
        0,
    ).astype(bf16)
    swap = [(i, i ^ 1) for i in range(n_ctx)]
    swap2 = [(i, i ^ 2) for i in range(n_ctx)]
    swap4 = [(i, i ^ 4) for i in range(n_ctx)]
    small = butterfly(
        small,
        [("context", swap), ("context", swap2), ("context", swap4), ("dp", [(0, 1), (1, 0)])],
        "cd",
    )
    cols = small[: 64 * 3].reshape(64, COLS)
    heads = small[64 * 3 :].astype(f32)
    q_up_all = heads[:32].reshape(16, 256)
    kv_up_all = heads[32:64].reshape(2, 16, 128)
    down_out_all = heads[64:96].reshape(16, 256)
    by_z = jnp.stack([cols, send(cols, ZF, "oz1"), send(cols, ZF2, "oz2"), send(cols, ZR, "oz3")])
    by_x = jnp.stack(
        [by_z, send(by_z, XP, "ox1"), send(by_z, X2, "ox2"), send(by_z, XM, "ox3")], 1
    ).reshape(16, 64, COLS)
    slot_t = jnp.stack([back[k] * 4 + (x - m) % 4 for k in range(4) for m in range(4)])
    pick = (slot_t[None, :] == jnp.arange(16, dtype=jnp.int32)[:, None]).astype(bf16)
    placed = dot(pick, by_x.reshape(16, 64 * COLS))
    placed = placed.reshape(16, 64, COLS)[: width // COLS].transpose(1, 0, 2).reshape(64, width)
    grad_down_qkv = placed[:48].reshape(3, 16, width)
    output_up_gradient = placed[48:]
    return (
        grad_input,
        grad_down_qkv,
        q_up_all,
        kv_up_all,
        down_out_all,
        output_up_gradient,
    )


def solution(mesh):
    in_specs = (
        P("dp", ("context", "tensor"), None),
        P("dp", ("context", "tensor"), None),
        P("dp", None),
        P(None, "tensor"),
        P(None, None, "tensor"),
        P("tensor", None),
        P(),
        P(None, "tensor"),
        P(None, None, "tensor"),
        P(None, "tensor"),
        P(),
    )
    out_specs = (
        P("dp", ("context", "tensor"), None),
        P(),
        P(None, "tensor"),
        P(None, None, "tensor"),
        P(None, "tensor"),
        P(),
    )
    return jax.shard_map(local, mesh=mesh, in_specs=in_specs, out_specs=out_specs, check_vma=False)
```

```python
import functools

import jax
import jax.numpy as jnp
import numpy as np
from jax import lax
from jax.experimental import pallas as pl
from jax.experimental.pallas import tpu as pltpu
from jax.sharding import PartitionSpec as P


HEAD_SIZE = 128
WINDOW = 1024
SHARD = 512
WIDTH = 5376
HALF = WIDTH // 2
AC = 1152
BC = WIDTH - AC
NB = 768
KC = 768
QB = 256

adapter_scale = 2.0
attn_scale = 168.0 ** (-0.5)
rope_base = 10000.0
bf16 = jnp.bfloat16
f32 = jnp.float32


NEXT = {0: 2, 2: 3, 3: 1, 1: 0}
PREV = {v: k for k, v in NEXT.items()}


def route(f):
    pairs = []
    for z in range(4):
        for x in range(4):
            a, b = f(z, x)
            pairs.append((z * 4 + x, a * 4 + b))
    return pairs


XP = route(lambda z, x: (z, (x + 1) % 4))
XM = route(lambda z, x: (z, (x - 1) % 4))
X2 = route(lambda z, x: (z, (x + 2) % 4))
ZF = route(lambda z, x: (NEXT[z], x))
ZR = route(lambda z, x: (PREV[z], x))
BX1 = route(lambda z, x: (z, x ^ 1))
BZ1 = route(lambda z, x: (z ^ 1, x))
BZ2 = route(lambda z, x: (z ^ 2, x))
BACK = np.zeros((4, 4), np.int32)
for z0 in range(4):
    at = z0
    for k0 in range(4):
        BACK[z0, k0] = at
        at = PREV[at]


def send(v, perm, axis="tensor"):
    return lax.ppermute(v, axis, perm)


def gather_pair(tokens, grads, ready):
    b = jnp.stack([tokens[:, AC:], grads[:, AC:]])
    a = jnp.stack([tokens[:, :AC], grads[:, :AC]])
    bs = [b]
    for _ in range(3):
        bs.append(send(bs[-1], ZF))
    a1 = send(a, XP)
    a3 = send(a, XM)
    a2 = send(a, X2)
    aparts = [jnp.stack([a, a1, a2, a3])]
    for _ in range(3):
        aparts.append(send(aparts[-1], ZF))
    halves = [aparts[:2], aparts[2:]]
    for g, own in enumerate((bs[0], bs[1], jnp.stack(bs[2:]))):
        left = send(own, XP)
        right = send(own, XM)
        if g == 0:
            left, *ready = lax.optimization_barrier((left, *ready))
        top = send(left[0], XP)
        bottom = send(right[1], XM)
        halves[g // 2] += [own, left, top, bottom, right]
    return halves, ready


def total(*terms):
    s = terms[0].astype(f32)
    for v in terms[1:]:
        s = s + v.astype(f32)
    return s.astype(bf16)


def scatter_rows(terms):
    done = [None] * 4
    for g in (1, 0):
        u0, u1, u2t, u2b, u3 = terms[g]
        s1 = send(u2t, XM)
        s2 = send(u2b, XP)
        u1 = u1.at[:32].set(total(u1[:32], s1))
        u3 = u3.at[32:].set(total(u3[32:], s2))
        v1 = send(u1, XM)
        v3 = send(u3, XP)
        done[2 * g] = total(u0[:32], v1[:32], v3[:32])
        done[2 * g + 1] = total(u0[32:], v1[32:], v3[32:])
    w = send(done[3], ZR)
    w = send(total(done[2], w), ZR)
    w = send(total(done[1], w), ZR)
    return total(done[0], w)


def assemble(which, parts, buf, sems):
    copies = []

    def put(src, i, m, first, width):
        dst = buf.at[pl.ds(128 * i + 32 * m, 32), pl.ds(first, width)]
        copies.append(pltpu.make_async_copy(src, dst, sems.at[16 * which + len(copies)]))

    for i in range(2):
        for m in range(4):
            put(parts[i].at[m, which], i, m, 0, AC)
        if len(parts) == 12:
            own, left, top, bottom, right = (
                p.at[which] if j in (0, 1, 4) else p for j, p in enumerate(parts[2 + 5 * i : 7 + 5 * i])
            )
            middle = (top, bottom)[which]
        else:
            own, left, top, bottom, right = (
                p.at[i, which] if j in (0, 1, 4) else p for j, p in enumerate(parts[2:])
            )
            middle = (top, bottom)[i].at[which]
        for m, src in enumerate((own, left, middle, right)):
            put(src, i, m, AC, BC)
    for copy in copies:
        copy.start()
    return copies


def turn(v, cos, sin):
    return v * cos + pltpu.roll(v, 64, 1) * sin


def input_kernel(half, *refs):
    n = 7 if half else 12
    parts, others, refs = refs[:n], refs[n : n + 10], refs[n + 10 :]
    wq, wkv, down, up_q, up_kv, cos, sin, w_out, up_out, down_out = others
    prev, refs = refs[: 5 * half], refs[5 * half :]
    q, kv, low, d_out, up, buf, g_buf, acc, acc_low, acc_out, acc_up, sems = refs
    copies = assemble(0, parts, buf, sems)
    g_copies = assemble(1, parts, g_buf, sems)
    if half:
        q[:256] = prev[0][...]
        kv[:, :256] = prev[1][...]
        low[:256] = prev[2][...]
        d_out[:256] = prev[3][...]
        up[:256] = prev[4][...]
    for total_ref in (acc, acc_low, acc_out, acc_up):
        total_ref[...] = jnp.zeros_like(total_ref)
    for copy in copies + g_copies:
        copy.wait()

    def step(i, carry):
        at = pl.ds(pl.multiple_of(i * KC, KC), KC)
        x = buf[:, at]
        acc[:, :256] += dot(x, wq[at, :])
        acc[:, 256:384] += dot(x, wkv[0, at, :])
        acc[:, 384:] += dot(x, wkv[1, at, :])
        acc_low[...] += dot_t(x, down[:, at])
        g = g_buf[:, at]
        acc_out[...] += dot_t(g, w_out[:, at])
        acc_up[...] += dot_t(g, up_out[:, at])
        return carry

    lax.fori_loop(0, WIDTH // KC, step, 0)
    rows = slice(256 * half, 256 * half + 256)
    adapted = acc_low[...].astype(bf16)
    low[rows] = adapted
    c, s = cos[rows], sin[rows]
    more = adapter_scale * dot(adapted[:, :16], up_q[...])
    for h in range(2):
        at = slice(128 * h, 128 * h + 128)
        q[rows, at] = turn(acc[:, at] + more[:, at], c, s).astype(bf16)
    more = adapter_scale * dot(adapted[:, 16:32], up_kv[0])
    kv[0, rows] = turn(acc[:, 256:384] + more, c, s).astype(bf16)
    more = adapter_scale * dot(adapted[:, 32:48], up_kv[1])
    kv[1, rows] = (acc[:, 384:512] + more).astype(bf16)
    up_grad = (adapter_scale * acc_up[...]).astype(bf16)
    up[rows] = up_grad
    d_out[rows] = (acc_out[...] + dot(up_grad, down_out[...])).astype(bf16)


def project_input(half, parts, others, prev):
    n = 256 * (half + 1)
    outs = [(n, 256), (2, n, 128), (n, 48), (n, 256), (n, 16)]
    hbm = pl.BlockSpec(memory_space=pl.ANY)
    vmem = pl.BlockSpec(memory_space=pltpu.VMEM)
    parts = [pltpu.with_memory_space_constraint(p, pltpu.HBM) for p in parts]
    res = pl.pallas_call(
        functools.partial(input_kernel, half),
        in_specs=[hbm] * len(parts) + [vmem] * (len(others) + len(prev)),
        out_specs=[vmem] * 7,
        out_shape=[jax.ShapeDtypeStruct(s, bf16) for s in outs + [(256, WIDTH)] * 2],
        scratch_shapes=[pltpu.VMEM((256, w), f32) for w in (512, 48, 256, 16)]
        + [pltpu.SemaphoreType.DMA((32,))],
        cost_estimate=pl.CostEstimate(
            flops=512 * WIDTH * 560, bytes_accessed=9_000_000, transcendentals=0
        ),
        compiler_params=pltpu.CompilerParams(vmem_limit_bytes=22 * 2**20),
    )(*parts, *others, *prev)
    return tuple(res[:5]), res[5], res[6]


def position(where, row):
    k = row >> 7
    z = jnp.where(k == 0, where[2], jnp.where(k == 1, where[3], jnp.where(k == 2, where[4], where[5])))
    m = (row >> 5) & 3
    return where[0] + (z * 4 + ((where[1] - m) & 3)) * 32 + (row & 31)


def attention_kernel(
    where, q, kv_own, kv_1, kv_2, d_out, low_rank, up_grad, down_o, up_q, cos, sin, *refs
):
    attended, dq, far, near, own, factor, hidden, q_up, down_out, kbuf, vbuf, dk, dv = refs
    for i, kv in enumerate((kv_2, kv_1, kv_own)):
        kbuf[512 * i : 512 * i + 512] = kv[0]
        vbuf[512 * i : 512 * i + 512] = kv[1]
    dk[...] = jnp.zeros_like(dk)
    dv[...] = jnp.zeros_like(dv)
    key = lax.broadcasted_iota(jnp.int32, (1, 3 * SHARD), 1)
    key_pos = position(where, key & (SHARD - 1)) + ((key >> 9) - 2) * SHARD

    def block(i, carry):
        at = pl.ds(pl.multiple_of(i * QB, QB), QB)
        pos = position(where, i * QB + lax.broadcasted_iota(jnp.int32, (QB, 1), 0))
        low = jnp.maximum(pos - (WINDOW - 1), 0)
        for v in (6, 7, 8):
            low = jnp.maximum(low, jnp.where(where[v] <= pos, where[v], 0))
        allowed = (key_pos >= low) & (key_pos <= pos)
        c, sn = cos[at, :], sin[at, :]
        for h in range(2):
            head = slice(128 * h, 128 * h + 128)
            qb, do = q[at, head], d_out[at, head]
            scores = jnp.where(allowed, dot_t(qb, kbuf[...]) * attn_scale, -1e30)
            e = jnp.exp(scores - jnp.max(scores, -1, keepdims=True))
            w = e * (1.0 / jnp.sum(e, -1, keepdims=True))
            wl = w.astype(bf16)
            att = dot(wl, vbuf[...]).astype(bf16)
            attended[at, head] = att
            row = jnp.sum(do.astype(f32) * att.astype(f32), -1, keepdims=True)
            ds = (w * (dot_t(do, vbuf[...]) - row) * attn_scale).astype(bf16)
            dq[at, head] = turn(dot(ds, kbuf[...]), c, -sn).astype(bf16)
            dk[...] += t_dot(ds, qb)
            dv[...] += t_dot(wl, do)
        return carry

    lax.fori_loop(0, SHARD // QB, block, 0)
    for i, acc in enumerate((dk, dv)):
        far[i] = acc[:512].astype(bf16)
        near[i] = acc[512:1024].astype(bf16)
        own[i] = acc[1024:]
    factor[...] = dot_t(attended[...], down_o[...]).astype(bf16)
    hidden[...] = (adapter_scale * dot_t(dq[...], up_q[...])).astype(bf16)
    q_up[...] = adapter_scale * t_dot(low_rank[:, :16], dq[...])
    down_out[...] = t_dot(up_grad[...], attended[...])


def attention(*args):
    vmem = pl.BlockSpec(memory_space=pltpu.VMEM)
    n = SHARD
    outs = [((n, 256), bf16)] * 2 + [((2, n, 128), bf16)] * 2 + [((2, n, 128), f32)]
    outs += [((n, 16), bf16)] * 2 + [((16, 256), f32)] * 2
    return pl.pallas_call(
        attention_kernel,
        in_specs=[pl.BlockSpec(memory_space=pltpu.SMEM)] + [vmem] * (len(args) - 1),
        out_specs=[vmem] * len(outs),
        out_shape=[jax.ShapeDtypeStruct(*o) for o in outs],
        scratch_shapes=[pltpu.VMEM((3 * n, 128), bf16)] * 2 + [pltpu.VMEM((3 * n, 128), f32)] * 2,
        cost_estimate=pl.CostEstimate(
            flops=14 * 2 * n * 3 * n * 128, bytes_accessed=4_000_000, transcendentals=0
        ),
        compiler_params=pltpu.CompilerParams(vmem_limit_bytes=22 * 2**20),
        name="attention",
    )(*args)


def finish_kernel(own, far, near, hq, low_rank, q_up, down_out, up_part, up_kv, cos, sin, x0, x1, *refs):
    lhs, hidden, sums = refs
    dk = own[0] + far[0].astype(f32) + near[0].astype(f32)
    dk = turn(dk, cos[...], -sin[...]).astype(bf16)
    dv = (own[1] + far[1].astype(f32) + near[1].astype(f32)).astype(bf16)
    lhs[:, :128] = dk
    lhs[:, 128:] = dv
    hidden[:, :16] = hq[...]
    hidden[:, 16:32] = (adapter_scale * dot_t(dk, up_kv[0])).astype(bf16)
    hidden[:, 32:48] = (adapter_scale * dot_t(dv, up_kv[1])).astype(bf16)
    for half in range(2):
        for j in range(3):
            at = slice(HALF * half + 896 * j, HALF * half + 896 * j + 896)
            to = slice(896 * j, 896 * j + 896)
            part = t_dot(hidden[:256], x0[:, at]) + t_dot(hidden[256:], x1[:, at])
            sums[64 * half : 64 * half + 48, to] = part.astype(bf16)
        sums[64 * half + 48 : 64 * half + 64, :HALF] = up_part[
            :, HALF * half : HALF * half + HALF
        ].astype(bf16)
    heads = [
        q_up[:, :128],
        q_up[:, 128:],
        adapter_scale * t_dot(low_rank[:, 16:32], dk),
        adapter_scale * t_dot(low_rank[:, 32:48], dv),
        down_out[:, :128],
        down_out[:, 128:],
        jnp.zeros((32, 128), f32),
    ]
    sums[:, HALF:] = jnp.concatenate(heads).astype(bf16)


def finish(*args):
    vmem = pl.BlockSpec(memory_space=pltpu.VMEM)
    outs = [(SHARD, 256), (SHARD, 48), (128, HALF + 128)]
    return pl.pallas_call(
        finish_kernel,
        in_specs=[vmem] * len(args),
        out_specs=[vmem] * len(outs),
        out_shape=[jax.ShapeDtypeStruct(o, bf16) for o in outs],
        cost_estimate=pl.CostEstimate(
            flops=2 * SHARD * WIDTH * 48, bytes_accessed=8_000_000, transcendentals=0
        ),
        compiler_params=pltpu.CompilerParams(vmem_limit_bytes=12 * 2**20),
        name="finish",
    )(*args)


def term_kernel(g, wq, wkv, dq, dkv, hidden, down, u0, u1, u2t, u2b, u3):
    half = slice(256 * g, 256 * g + 256)

    def step(j, carry):
        at = pl.ds(pl.multiple_of(j * NB, NB), NB)
        res = dot_t(dq[half], wq[at, :]) + dot_t(dkv[half, :128], wkv[0, at, :])
        res = res + dot_t(dkv[half, 128:], wkv[1, at, :]) + dot(hidden[half], down[:, at])
        res = res.astype(bf16)
        for i in range(2):
            row = 128 * i
            rows = slice(32 * i, 32 * i + 32)
            u0[rows, at] = res[row : row + 32]
            u1[rows, at] = res[row + 32 : row + 64]
            (u2t, u2b)[i][:, at] = res[row + 64 : row + 96]
            u3[rows, at] = res[row + 96 : row + 128]
        return carry

    lax.fori_loop(0, WIDTH // NB, step, 0)


def term_parts(g, *args):
    vmem = pl.BlockSpec(memory_space=pltpu.VMEM)
    return pl.pallas_call(
        functools.partial(term_kernel, g),
        in_specs=[vmem] * len(args),
        out_specs=[vmem] * 5,
        out_shape=[jax.ShapeDtypeStruct((r, WIDTH), bf16) for r in (64, 64, 32, 32, 64)],
        cost_estimate=pl.CostEstimate(
            flops=SHARD * WIDTH * 560, bytes_accessed=9_000_000, transcendentals=0
        ),
        compiler_params=pltpu.CompilerParams(vmem_limit_bytes=16 * 2**20),
    )(*args)


def halve(v, bit, axis, perm):
    n = v.shape[0] // 2
    away = jnp.where(bit == 1, v[:n], v[n:])
    kept = jnp.where(bit == 1, v[n:], v[:n])
    return total(kept, send(away, perm, axis))


def widen(v, bit, axis, perm):
    w = send(v, perm, axis)
    first = jnp.where(bit == 1, w, v)
    second = jnp.where(bit == 1, v, w)
    return jnp.concatenate([first, second])


def butterfly(v, steps):
    for axis, perm in steps:
        v = lax.optimization_barrier(v)
        v = total(v, send(v, perm, axis))
    return v


def dot(a, b):
    return jnp.dot(a, b, preferred_element_type=f32)


def dot_t(a, b):
    return lax.dot_general(a, b, (((1,), (1,)), ((), ())), preferred_element_type=f32)


def t_dot(a, b):
    return lax.dot_general(a, b, (((0,), (0,)), ((), ())), preferred_element_type=f32)


def body(
    tokens,
    output_gradient,
    document_index,
    query_weight,
    key_value_weight,
    output_weight,
    adapter_down_projections,
    adapter_up_query,
    adapter_up_key_value,
    adapter_down_output,
    adapter_up_output,
):
    c = lax.axis_index("context")
    t = lax.axis_index("tensor")
    z, x = t // 4, t % 4
    width = tokens.shape[2]
    shard = SHARD
    n_ctx = lax.axis_size("context")

    back = jnp.asarray(BACK)[z]
    seg = document_index[0]
    starts = [jnp.sum((seg < v).astype(jnp.int32)) for v in (1, 2, 3)]
    at = jnp.arange(9, dtype=jnp.int32)
    where = jnp.zeros(9, jnp.int32)
    for i, v in enumerate([c * shard, x, *[back[k] for k in range(4)], *starts]):
        where = jnp.where(at == i, v, where)
    q_pos = position(where, jnp.arange(shard, dtype=jnp.int32))
    inverse = rope_base ** (-(jnp.arange(64, dtype=f32) * 2.0 / HEAD_SIZE))
    angle = q_pos.astype(f32)[:, None] * inverse[None, :]
    cos, sin = jnp.cos(angle), jnp.sin(angle)

    down_all = adapter_down_projections.reshape(48, width)

    cos_all = jnp.concatenate([cos, cos], 1)
    sin_all = jnp.concatenate([-sin, sin], 1)
    ready = [where, cos_all, sin_all]
    halves, ready = gather_pair(tokens[0], output_gradient[0], ready)
    where, cos_all, sin_all = ready
    others = (
        query_weight,
        key_value_weight,
        down_all,
        adapter_up_query,
        adapter_up_key_value,
        cos_all,
        sin_all,
        output_weight,
        adapter_up_output,
        adapter_down_output,
    )
    prev, x0, g0 = project_input(0, halves[0], others, ())
    (q_all, kv_own, adapted, d_out, up_grad), x1, g1 = project_input(1, halves[1], others, prev)
    kv_1 = send(kv_own, [(i, i + 1) for i in range(n_ctx - 1)], "context")
    kv_2 = send(kv_own, [(i, i + 2) for i in range(n_ctx - 2)], "context")
    res = attention(
        where,
        q_all,
        kv_own,
        kv_1,
        kv_2,
        d_out,
        adapted,
        up_grad,
        adapter_down_output,
        adapter_up_query,
        cos_all,
        sin_all,
    )
    _, d_q, far, near, own, factor, hidden_q, q_up, down_out = res
    far = send(far, [(i, i - 2) for i in range(2, n_ctx)], "context")
    near = send(near, [(i, i - 1) for i in range(1, n_ctx)], "context")
    up_part = adapter_scale * (t_dot(factor[:256], g0) + t_dot(factor[256:], g1))
    d_kv, hidden, sums = finish(
        own,
        far,
        near,
        hidden_q,
        adapted,
        q_up,
        down_out,
        up_part,
        adapter_up_key_value,
        cos_all,
        sin_all,
        x0,
        x1,
    )

    args = (query_weight, key_value_weight, d_q, d_kv, hidden, down_all)
    grad_input = scatter_rows([term_parts(0, *args), term_parts(1, *args)])[None]

    pairs = [("context", [(i, i ^ m) for i in range(n_ctx)], (c // m) % 2) for m in (1, 2, 4)]
    pairs.append(("dp", [(0, 1), (1, 0)], lax.axis_index("dp")))
    for axis, perm, bit in pairs:
        sums = halve(sums, bit, axis, perm)
    tops = butterfly(
        sums[:, :HALF], [("tensor", BZ1), ("tensor", BZ2), ("tensor", BX1), ("tensor", X2)]
    )
    sums = jnp.concatenate([tops, sums[:, HALF:]], 1)
    for axis, perm, bit in pairs[::-1]:
        sums = widen(sums, bit, axis, perm)
    sums = sums.astype(f32)
    wide = jnp.concatenate([sums[:64, :HALF], sums[64:, :HALF]], 1)
    heads = sums[:, HALF:]
    grad_down_qkv = wide[:48].reshape(3, 16, width)
    output_up_gradient = wide[48:]
    q_up_all = jnp.concatenate([heads[:16], heads[16:32]], 1)
    kv_up_all = heads[32:64].reshape(2, 16, 128)
    down_out_all = jnp.concatenate([heads[64:80], heads[80:96]], 1)
    return (
        grad_input,
        grad_down_qkv,
        q_up_all,
        kv_up_all,
        down_out_all,
        output_up_gradient,
    )


def solution(mesh):
    in_specs = (
        P("dp", ("context", "tensor"), None),
        P("dp", ("context", "tensor"), None),
        P("dp", None),
        P(None, "tensor"),
        P(None, None, "tensor"),
        P("tensor", None),
        P(),
        P(None, "tensor"),
        P(None, None, "tensor"),
        P(None, "tensor"),
        P(),
    )
    out_specs = (
        P("dp", ("context", "tensor"), None),
        P(),
        P(None, "tensor"),
        P(None, None, "tensor"),
        P(None, "tensor"),
        P(),
    )
    return jax.shard_map(body, mesh=mesh, in_specs=in_specs, out_specs=out_specs, check_vma=False)
```

```python
import functools

import jax
import jax.numpy as jnp
import numpy as np
from jax import lax
from jax.experimental import pallas as pl
from jax.experimental.pallas import tpu as pltpu
from jax.sharding import PartitionSpec as P


HEAD_SIZE = 128
WINDOW = 1024
SHARD = 512
WIDTH = 5376
HALF = WIDTH // 2
AC = 1152
BC = WIDTH - AC
NB = 768
KC = 768
QB = 256

adapter_scale = 2.0
attn_scale = 168.0 ** (-0.5)
rope_base = 10000.0
bf16 = jnp.bfloat16
f32 = jnp.float32


NEXT = {0: 2, 2: 3, 3: 1, 1: 0}
PREV = {v: k for k, v in NEXT.items()}


def route(f):
    pairs = []
    for z in range(4):
        for x in range(4):
            a, b = f(z, x)
            pairs.append((z * 4 + x, a * 4 + b))
    return pairs


XP = route(lambda z, x: (z, (x + 1) % 4))
XM = route(lambda z, x: (z, (x - 1) % 4))
X2 = route(lambda z, x: (z, (x + 2) % 4))
ZF = route(lambda z, x: (NEXT[z], x))
ZR = route(lambda z, x: (PREV[z], x))
BX1 = route(lambda z, x: (z, x ^ 1))
BZ1 = route(lambda z, x: (z ^ 1, x))
BZ2 = route(lambda z, x: (z ^ 2, x))
BACK = np.zeros((4, 4), np.int32)
for z0 in range(4):
    at = z0
    for k0 in range(4):
        BACK[z0, k0] = at
        at = PREV[at]


def send(v, perm, axis="tensor"):
    return lax.ppermute(v, axis, perm)


def gather_pair(tokens, grads):
    b = jnp.stack([tokens[:, AC:], grads[:, AC:]])
    a = jnp.stack([tokens[:, :AC], grads[:, :AC]])
    bs = [b]
    for _ in range(3):
        bs.append(send(bs[-1], ZF))
    a1 = send(a, XP)
    a3 = send(a, XM)
    a2 = send(a, X2)
    aparts = [jnp.stack([a, a1, a2, a3])]
    for _ in range(3):
        aparts.append(send(aparts[-1], ZF))
    halves = [aparts[:2], aparts[2:]]
    for g, own in enumerate((bs[0], bs[1], jnp.stack(bs[2:]))):
        left = send(own, XP)
        right = send(own, XM)
        first, second = left[0], right[1]
        top = send(first, XP)
        bottom = send(second, XM)
        halves[g // 2] += [own, left, top, bottom, right]
    return halves


def total(*terms):
    s = terms[0].astype(f32)
    for v in terms[1:]:
        s = s + v.astype(f32)
    return s.astype(bf16)


def scatter_rows(terms):
    done = [None] * 4
    for g in (1, 0):
        u0, u1, u2t, u2b, u3 = terms[g]
        s1 = send(u2t, XM)
        s2 = send(u2b, XP)
        u1 = u1.at[:32].set(total(u1[:32], s1))
        u3 = u3.at[32:].set(total(u3[32:], s2))
        v1 = send(u1, XM)
        v3 = send(u3, XP)
        done[2 * g] = total(u0[:32], v1[:32], v3[:32])
        done[2 * g + 1] = total(u0[32:], v1[32:], v3[32:])
    w = send(done[3], ZR)
    w = send(total(done[2], w), ZR)
    w = send(total(done[1], w), ZR)
    return total(done[0], w)


def assemble(which, parts, buf, sems):
    copies = []

    def put(src, i, m, first, width):
        dst = buf.at[pl.ds(128 * i + 32 * m, 32), pl.ds(first, width)]
        copies.append(pltpu.make_async_copy(src, dst, sems.at[16 * which + len(copies)]))

    for i in range(2):
        for m in range(4):
            put(parts[i].at[m, which], i, m, 0, AC)
        if len(parts) == 12:
            own, left, top, bottom, right = (
                p.at[which] if j in (0, 1, 4) else p for j, p in enumerate(parts[2 + 5 * i : 7 + 5 * i])
            )
            middle = (top, bottom)[which]
        else:
            own, left, top, bottom, right = (
                p.at[i, which] if j in (0, 1, 4) else p for j, p in enumerate(parts[2:])
            )
            middle = (top, bottom)[i].at[which]
        for m, src in enumerate((own, left, middle, right)):
            put(src, i, m, AC, BC)
    for copy in copies:
        copy.start()
    return copies


def turn(v, cos, sin):
    return v * cos + pltpu.roll(v, 64, 1) * sin


def input_kernel(half, *refs):
    n = 7 if half else 12
    parts, others, refs = refs[:n], refs[n : n + 10], refs[n + 10 :]
    wq, wkv, down, up_q, up_kv, cos, sin, w_out, up_out, down_out = others
    prev, refs = refs[: 5 * half], refs[5 * half :]
    q, kv, low, d_out, up, buf, g_buf, acc, acc_low, acc_out, acc_up, sems = refs
    copies = assemble(0, parts, buf, sems)
    g_copies = assemble(1, parts, g_buf, sems)
    if half:
        q[:256] = prev[0][...]
        kv[:, :256] = prev[1][...]
        low[:256] = prev[2][...]
        d_out[:256] = prev[3][...]
        up[:256] = prev[4][...]
    for total_ref in (acc, acc_low, acc_out, acc_up):
        total_ref[...] = jnp.zeros_like(total_ref)
    for copy in copies + g_copies:
        copy.wait()

    def step(i, carry):
        at = pl.ds(pl.multiple_of(i * KC, KC), KC)
        x = buf[:, at]
        acc[:, :256] += dot(x, wq[at, :])
        acc[:, 256:384] += dot(x, wkv[0, at, :])
        acc[:, 384:] += dot(x, wkv[1, at, :])
        acc_low[...] += dot_t(x, down[:, at])
        g = g_buf[:, at]
        acc_out[...] += dot_t(g, w_out[:, at])
        acc_up[...] += dot_t(g, up_out[:, at])
        return carry

    lax.fori_loop(0, WIDTH // KC, step, 0)
    rows = slice(256 * half, 256 * half + 256)
    adapted = acc_low[...].astype(bf16)
    low[rows] = adapted
    c, s = cos[rows], sin[rows]
    more = adapter_scale * dot(adapted[:, :16], up_q[...])
    for h in range(2):
        at = slice(128 * h, 128 * h + 128)
        q[rows, at] = turn(acc[:, at] + more[:, at], c, s).astype(bf16)
    more = adapter_scale * dot(adapted[:, 16:32], up_kv[0])
    kv[0, rows] = turn(acc[:, 256:384] + more, c, s).astype(bf16)
    more = adapter_scale * dot(adapted[:, 32:48], up_kv[1])
    kv[1, rows] = (acc[:, 384:512] + more).astype(bf16)
    up_grad = (adapter_scale * acc_up[...]).astype(bf16)
    up[rows] = up_grad
    d_out[rows] = (acc_out[...] + dot(up_grad, down_out[...])).astype(bf16)


def project_input(half, parts, others, prev):
    n = 256 * (half + 1)
    outs = [(n, 256), (2, n, 128), (n, 48), (n, 256), (n, 16)]
    hbm = pl.BlockSpec(memory_space=pl.ANY)
    vmem = pl.BlockSpec(memory_space=pltpu.VMEM)
    res = pl.pallas_call(
        functools.partial(input_kernel, half),
        in_specs=[hbm] * len(parts) + [vmem] * (len(others) + len(prev)),
        out_specs=[vmem] * 7,
        out_shape=[pltpu.HBM(s, bf16) for s in outs + [(256, WIDTH)] * 2],
        scratch_shapes=[pltpu.VMEM((256, w), f32) for w in (512, 48, 256, 16)]
        + [pltpu.SemaphoreType.DMA((32,))],
        cost_estimate=pl.CostEstimate(
            flops=512 * WIDTH * 560, bytes_accessed=9_000_000, transcendentals=0
        ),
        compiler_params=pltpu.CompilerParams(vmem_limit_bytes=22 * 2**20),
    )(*in_hbm(parts), *others, *in_hbm(prev))
    return tuple(res[:5]), res[5], res[6]


def position(where, row):
    k = row >> 7
    z = jnp.where(k == 0, where[2], jnp.where(k == 1, where[3], jnp.where(k == 2, where[4], where[5])))
    m = (row >> 5) & 3
    return where[0] + (z * 4 + ((where[1] - m) & 3)) * 32 + (row & 31)


def attention_kernel(
    where, q, kv_own, kv_1, kv_2, d_out, low_rank, up_grad, down_o, up_q, cos, sin, *refs
):
    attended, dq, far, near, own, factor, hidden, q_up, down_out, kbuf, vbuf, dk, dv = refs
    for i, kv in enumerate((kv_2, kv_1, kv_own)):
        kbuf[512 * i : 512 * i + 512] = kv[0]
        vbuf[512 * i : 512 * i + 512] = kv[1]
    dk[...] = jnp.zeros_like(dk)
    dv[...] = jnp.zeros_like(dv)
    key = lax.broadcasted_iota(jnp.int32, (1, 3 * SHARD), 1)
    key_pos = position(where, key & (SHARD - 1)) + ((key >> 9) - 2) * SHARD

    def block(i, carry):
        at = pl.ds(pl.multiple_of(i * QB, QB), QB)
        pos = position(where, i * QB + lax.broadcasted_iota(jnp.int32, (QB, 1), 0))
        low = jnp.maximum(pos - (WINDOW - 1), 0)
        for v in (6, 7, 8):
            low = jnp.maximum(low, jnp.where(where[v] <= pos, where[v], 0))
        allowed = (key_pos >= low) & (key_pos <= pos)
        c, sn = cos[at, :], sin[at, :]
        for h in range(2):
            head = slice(128 * h, 128 * h + 128)
            qb, do = q[at, head], d_out[at, head]
            scores = jnp.where(allowed, dot_t(qb, kbuf[...]) * attn_scale, -1e30)
            e = jnp.exp(scores - jnp.max(scores, -1, keepdims=True))
            w = e * (1.0 / jnp.sum(e, -1, keepdims=True))
            wl = w.astype(bf16)
            att = dot(wl, vbuf[...]).astype(bf16)
            attended[at, head] = att
            row = jnp.sum(do.astype(f32) * att.astype(f32), -1, keepdims=True)
            ds = (w * (dot_t(do, vbuf[...]) - row) * attn_scale).astype(bf16)
            dq[at, head] = turn(dot(ds, kbuf[...]), c, -sn).astype(bf16)
            dk[...] += t_dot(ds, qb)
            dv[...] += t_dot(wl, do)
        return carry

    lax.fori_loop(0, SHARD // QB, block, 0)
    for i, acc in enumerate((dk, dv)):
        far[i] = acc[:512].astype(bf16)
        near[i] = acc[512:1024].astype(bf16)
        own[i] = acc[1024:]
    factor[...] = dot_t(attended[...], down_o[...]).astype(bf16)
    hidden[...] = (adapter_scale * dot_t(dq[...], up_q[...])).astype(bf16)
    q_up[...] = adapter_scale * t_dot(low_rank[:, :16], dq[...])
    down_out[...] = t_dot(up_grad[...], attended[...])


def in_hbm(args):
    return [pltpu.with_memory_space_constraint(v, pltpu.HBM) for v in args]


def attention(where, *args):
    vmem = pl.BlockSpec(memory_space=pltpu.VMEM)
    n = SHARD
    outs = [((n, 256), bf16)] * 2 + [((2, n, 128), bf16)] * 2 + [((2, n, 128), f32)]
    outs += [((n, 16), bf16)] * 2 + [((16, 256), f32)] * 2
    return pl.pallas_call(
        attention_kernel,
        in_specs=[pl.BlockSpec(memory_space=pltpu.SMEM)] + [vmem] * len(args),
        out_specs=[vmem] * len(outs),
        out_shape=[pltpu.HBM(*o) for o in outs],
        scratch_shapes=[pltpu.VMEM((3 * n, 128), bf16)] * 2 + [pltpu.VMEM((3 * n, 128), f32)] * 2,
        cost_estimate=pl.CostEstimate(
            flops=14 * 2 * n * 3 * n * 128, bytes_accessed=4_000_000, transcendentals=0
        ),
        compiler_params=pltpu.CompilerParams(vmem_limit_bytes=22 * 2**20),
        name="attention",
    )(where, *in_hbm(args))


def finish_kernel(own, far, near, hq, low_rank, q_up, down_out, up_part, up_kv, cos, sin, x0, x1, *refs):
    lhs, hidden, sums = refs
    dk = own[0] + far[0].astype(f32) + near[0].astype(f32)
    dk = turn(dk, cos[...], -sin[...]).astype(bf16)
    dv = (own[1] + far[1].astype(f32) + near[1].astype(f32)).astype(bf16)
    lhs[:, :128] = dk
    lhs[:, 128:] = dv
    hidden[:, :16] = hq[...]
    hidden[:, 16:32] = (adapter_scale * dot_t(dk, up_kv[0])).astype(bf16)
    hidden[:, 32:48] = (adapter_scale * dot_t(dv, up_kv[1])).astype(bf16)
    for half in range(2):
        for j in range(3):
            at = slice(HALF * half + 896 * j, HALF * half + 896 * j + 896)
            to = slice(896 * j, 896 * j + 896)
            part = t_dot(hidden[:256], x0[:, at]) + t_dot(hidden[256:], x1[:, at])
            sums[64 * half : 64 * half + 48, to] = part.astype(bf16)
        sums[64 * half + 48 : 64 * half + 64, :HALF] = up_part[
            :, HALF * half : HALF * half + HALF
        ].astype(bf16)
    heads = [
        q_up[:, :128],
        q_up[:, 128:],
        adapter_scale * t_dot(low_rank[:, 16:32], dk),
        adapter_scale * t_dot(low_rank[:, 32:48], dv),
        down_out[:, :128],
        down_out[:, 128:],
        jnp.zeros((32, 128), f32),
    ]
    sums[:, HALF:] = jnp.concatenate(heads).astype(bf16)


def finish(*args):
    vmem = pl.BlockSpec(memory_space=pltpu.VMEM)
    outs = [(SHARD, 256), (SHARD, 48), (128, HALF + 128)]
    return pl.pallas_call(
        finish_kernel,
        in_specs=[vmem] * len(args),
        out_specs=[vmem] * len(outs),
        out_shape=[pltpu.HBM(o, bf16) for o in outs],
        cost_estimate=pl.CostEstimate(
            flops=2 * SHARD * WIDTH * 48, bytes_accessed=8_000_000, transcendentals=0
        ),
        compiler_params=pltpu.CompilerParams(vmem_limit_bytes=12 * 2**20),
        name="finish",
    )(*in_hbm(args[:-2]), *args[-2:])


def term_kernel(g, wq, wkv, dq, dkv, hidden, down, u0, u1, u2t, u2b, u3):
    half = slice(256 * g, 256 * g + 256)

    def step(j, carry):
        at = pl.ds(pl.multiple_of(j * NB, NB), NB)
        res = dot_t(dq[half], wq[at, :]) + dot_t(dkv[half, :128], wkv[0, at, :])
        res = res + dot_t(dkv[half, 128:], wkv[1, at, :]) + dot(hidden[half], down[:, at])
        res = res.astype(bf16)
        for i in range(2):
            row = 128 * i
            rows = slice(32 * i, 32 * i + 32)
            u0[rows, at] = res[row : row + 32]
            u1[rows, at] = res[row + 32 : row + 64]
            (u2t, u2b)[i][:, at] = res[row + 64 : row + 96]
            u3[rows, at] = res[row + 96 : row + 128]
        return carry

    lax.fori_loop(0, WIDTH // NB, step, 0)


def term_parts(g, wq, wkv, dq, dkv, hidden, down):
    vmem = pl.BlockSpec(memory_space=pltpu.VMEM)
    return pl.pallas_call(
        functools.partial(term_kernel, g),
        in_specs=[vmem] * 6,
        out_specs=[vmem] * 5,
        out_shape=[jax.ShapeDtypeStruct((r, WIDTH), bf16) for r in (64, 64, 32, 32, 64)],
        cost_estimate=pl.CostEstimate(
            flops=SHARD * WIDTH * 560, bytes_accessed=9_000_000, transcendentals=0
        ),
        compiler_params=pltpu.CompilerParams(vmem_limit_bytes=16 * 2**20),
    )(wq, wkv, *in_hbm((dq, dkv, hidden)), down)


def halve(v, bit, axis, perm):
    n = v.shape[0] // 2
    away = jnp.where(bit == 1, v[:n], v[n:])
    kept = jnp.where(bit == 1, v[n:], v[:n])
    return total(kept, send(away, perm, axis))


def widen(v, bit, axis, perm):
    w = send(v, perm, axis)
    first = jnp.where(bit == 1, w, v)
    second = jnp.where(bit == 1, v, w)
    return jnp.concatenate([first, second])


def butterfly(v, steps):
    for axis, perm in steps:
        v = lax.optimization_barrier(v)
        v = total(v, send(v, perm, axis))
    return v


def dot(a, b):
    return jnp.dot(a, b, preferred_element_type=f32)


def dot_t(a, b):
    return lax.dot_general(a, b, (((1,), (1,)), ((), ())), preferred_element_type=f32)


def t_dot(a, b):
    return lax.dot_general(a, b, (((0,), (0,)), ((), ())), preferred_element_type=f32)


def body(
    tokens,
    output_gradient,
    document_index,
    query_weight,
    key_value_weight,
    output_weight,
    adapter_down_projections,
    adapter_up_query,
    adapter_up_key_value,
    adapter_down_output,
    adapter_up_output,
):
    c = lax.axis_index("context")
    t = lax.axis_index("tensor")
    z, x = t // 4, t % 4
    width = tokens.shape[2]
    shard = SHARD
    n_ctx = lax.axis_size("context")

    def prepare():
        back = jnp.asarray(BACK)[z]
        seg = document_index[0]
        starts = [jnp.sum((seg < v).astype(jnp.int32)) for v in (1, 2, 3)]
        at = jnp.arange(9, dtype=jnp.int32)
        where = jnp.zeros(9, jnp.int32)
        for i, v in enumerate([c * shard, x, *[back[k] for k in range(4)], *starts]):
            where = jnp.where(at == i, v, where)
        q_pos = position(where, jnp.arange(shard, dtype=jnp.int32))
        inverse = rope_base ** (-(jnp.arange(64, dtype=f32) * 2.0 / HEAD_SIZE))
        angle = q_pos.astype(f32)[:, None] * inverse[None, :]
        cos, sin = jnp.cos(angle), jnp.sin(angle)
        return where, jnp.concatenate([cos, cos], 1), jnp.concatenate([-sin, sin], 1)

    down_all = adapter_down_projections.reshape(48, width)

    where, cos_all, sin_all = prepare()
    halves = gather_pair(tokens[0], output_gradient[0])
    others = (
        query_weight,
        key_value_weight,
        down_all,
        adapter_up_query,
        adapter_up_key_value,
        cos_all,
        sin_all,
        output_weight,
        adapter_up_output,
        adapter_down_output,
    )
    prev, x0, g0 = project_input(0, halves[0], others, ())
    (q_all, kv_own, adapted, d_out, up_grad), x1, g1 = project_input(1, halves[1], others, prev)
    kv_1 = send(kv_own, [(i, i + 1) for i in range(n_ctx - 1)], "context")
    kv_2 = send(kv_own, [(i, i + 2) for i in range(n_ctx - 2)], "context")
    res = attention(
        where,
        q_all,
        kv_own,
        kv_1,
        kv_2,
        d_out,
        adapted,
        up_grad,
        adapter_down_output,
        adapter_up_query,
        cos_all,
        sin_all,
    )
    _, d_q, far, near, own, factor, hidden_q, q_up, down_out = res
    far = send(far, [(i, i - 2) for i in range(2, n_ctx)], "context")
    near = send(near, [(i, i - 1) for i in range(1, n_ctx)], "context")
    up_part = adapter_scale * (t_dot(factor[:256], g0) + t_dot(factor[256:], g1))
    d_kv, hidden, sums = finish(
        own,
        far,
        near,
        hidden_q,
        adapted,
        q_up,
        down_out,
        up_part,
        adapter_up_key_value,
        cos_all,
        sin_all,
        x0,
        x1,
    )

    args = (query_weight, key_value_weight, d_q, d_kv, hidden, down_all)
    grad_input = scatter_rows([term_parts(0, *args), term_parts(1, *args)])[None]

    pairs = [("context", [(i, i ^ m) for i in range(n_ctx)], (c // m) % 2) for m in (1, 2, 4)]
    pairs.append(("dp", [(0, 1), (1, 0)], lax.axis_index("dp")))
    for axis, perm, bit in pairs:
        sums = halve(sums, bit, axis, perm)
    tops = butterfly(
        sums[:, :HALF], [("tensor", BZ1), ("tensor", BZ2), ("tensor", BX1), ("tensor", X2)]
    )
    sums = jnp.concatenate([tops, sums[:, HALF:]], 1)
    for axis, perm, bit in pairs[::-1]:
        sums = widen(sums, bit, axis, perm)
    sums = sums.astype(f32)
    wide = jnp.concatenate([sums[:64, :HALF], sums[64:, :HALF]], 1)
    heads = sums[:, HALF:]
    grad_down_qkv = wide[:48].reshape(3, 16, width)
    output_up_gradient = wide[48:]
    q_up_all = jnp.concatenate([heads[:16], heads[16:32]], 1)
    kv_up_all = heads[32:64].reshape(2, 16, 128)
    down_out_all = jnp.concatenate([heads[64:80], heads[80:96]], 1)
    return (
        grad_input,
        grad_down_qkv,
        q_up_all,
        kv_up_all,
        down_out_all,
        output_up_gradient,
    )


def solution(mesh):
    in_specs = (
        P("dp", ("context", "tensor"), None),
        P("dp", ("context", "tensor"), None),
        P("dp", None),
        P(None, "tensor"),
        P(None, None, "tensor"),
        P("tensor", None),
        P(),
        P(None, "tensor"),
        P(None, None, "tensor"),
        P(None, "tensor"),
        P(),
    )
    out_specs = (
        P("dp", ("context", "tensor"), None),
        P(),
        P(None, "tensor"),
        P(None, None, "tensor"),
        P(None, "tensor"),
        P(),
    )
    return jax.shard_map(body, mesh=mesh, in_specs=in_specs, out_specs=out_specs, check_vma=False)
```
